32 devices in a mesh: gx: 4 (over z), gy: 4 (over x, core), tracer: 2 (over y).
Axes of the slice: x: 2, y: 2, z: 4, core: 2. Of those that a mesh axis runs over, the one named last changes fastest.
Arguments:
- biology_concentration: float32 [24, 8, 256, 512], P('tracer', None, 'gy', 'gx'), may hold values from 0.1 to 2
- flow_vectors: float32 [2, 8, 256, 512], P(None, 'tracer', 'gy', 'gx'), may hold values from -0.25 to 0.25
- thermal_anomaly: float32 [8, 256, 512], P('tracer', 'gy', 'gx'), may hold values from -6 to 6
- diffusivity_profile: float32 [8, 256, 512], P(None, 'gy', 'gx'), may hold values from 0.02 to 0.24
- solar_flux_field: float32 [256, 512], P('gy', 'gx'), may hold values from 0.5 to 2
- ecosystem_coefficients: float32 [24], P('tracer'), may hold values from 0.05 to 0.5
- ocean_indicator: int32 [256, 512], P('gy', 'gx'), may hold values 0 or 1
- floor_tier_number: int32 [256, 512], P('gy', 'gx'), may hold values from 1 to 8
Outputs:
- tracers_out: float32 [24, 8, 256, 512], P('tracer', None, 'gy', 'gx')
- currents_out: float32 [2, 8, 256, 512], P(None, 'tracer', 'gy', 'gx')
- temperature_out: float32 [8, 256, 512], P('tracer', 'gy', 'gx')
The draws below stay inside these ranges and needn't reach their ends.
All inputs are finite; a program needn't handle non-finite values. No bound on the sum of `ocean_indicator` on one device may be relied on, other than what follows from the above.
Results may differ from the reference program's by a relative error of at most 0.0003.
Values sent between devices are 32-bit elements; how exact they have to be, the bound alone decides.
A program may use at most 64 MiB of HBM per device.

```python
import math
import jax
import jax.numpy as jnp

NTR = 24
VERTICAL_TIERS = 8
STEPS = 2
MESH_LONGITUDES = 512
MESH_LATITUDES = 256


def set_ends(entries, rng, low, high):
    spot = [jax.random.randint(jax.random.fold_in(rng, axis), (), 0, length) for axis, length in enumerate(entries.shape)]
    widest = entries.shape.index(max(entries.shape))
    neighbour = spot[:widest] + [(spot[widest] + 1) % entries.shape[widest]] + spot[widest + 1:]
    return entries.at[tuple(spot)].set(low).at[tuple(neighbour)].set(high)


def block_scale(stream_key, extent, pieces, least, high):
    loudness, own = 1.0, jax.random.fold_in(stream_key, 6)
    for position, blocks in pieces:
        steps = jnp.exp(jax.random.uniform(jax.random.fold_in(own, position), (blocks,), jnp.float32, least / len(pieces), high / len(pieces)))
        loudness = loudness * jnp.repeat(steps, extent[position] // blocks).reshape([-1 if axis == position else 1 for axis in range(len(extent))])
    return loudness


def noise(stream_key, extent, width, bound, shards=(), kind=jnp.bfloat16):
    factor_of = block_scale(stream_key, extent, shards, -0.22, 0.18) if shards else 1.0
    values = jax.random.normal(stream_key, extent, jnp.float32) * width * factor_of
    return jnp.minimum(jnp.maximum(values, -bound), bound).astype(kind)


def setup_inputs(seed: int = 0) -> dict:
    seeds = jax.random.split(jax.random.key(seed), 9)
    return {
        "biology_concentration": jnp.clip(jnp.exp(math.log(2.0) - 2.9957323 * jax.random.uniform(seeds[0], (NTR, VERTICAL_TIERS, MESH_LATITUDES, MESH_LONGITUDES), jnp.float32) ** block_scale(seeds[0], (NTR, VERTICAL_TIERS, MESH_LATITUDES, MESH_LONGITUDES), ((0, 2), (2, 4), (3, 4)), -0.2, 0.2)), 0.1, 2.0),
        "flow_vectors": jnp.clip(jax.random.uniform(seeds[1], (2, VERTICAL_TIERS, MESH_LATITUDES, MESH_LONGITUDES), jnp.float32, -0.25, 0.25) * block_scale(seeds[1], (2, VERTICAL_TIERS, MESH_LATITUDES, MESH_LONGITUDES), ((1, 2), (2, 4), (3, 4)), -0.4, 0.0), -0.25, 0.25),
        "thermal_anomaly": noise(seeds[2], (VERTICAL_TIERS, MESH_LATITUDES, MESH_LONGITUDES), 1.0, 6.0, ((0, 2), (1, 4), (2, 4)), jnp.float32),
        "diffusivity_profile": jnp.clip(jnp.exp(math.log(0.24) - 2.4849066 * jax.random.uniform(seeds[3], (VERTICAL_TIERS, MESH_LATITUDES, MESH_LONGITUDES), jnp.float32) ** block_scale(seeds[3], (VERTICAL_TIERS, MESH_LATITUDES, MESH_LONGITUDES), ((1, 4), (2, 4)), -0.2, 0.2)), 0.02, 0.24),
        "solar_flux_field": jnp.clip(jnp.exp(math.log(2.0) - 1.3862944 * jax.random.uniform(seeds[4], (MESH_LATITUDES, MESH_LONGITUDES), jnp.float32) ** block_scale(seeds[4], (MESH_LATITUDES, MESH_LONGITUDES), ((0, 4), (1, 4)), -0.2, 0.2)), 0.5, 2.0),
        "ecosystem_coefficients": jnp.clip(jnp.exp(math.log(0.5) - 2.3025851 * jax.random.uniform(seeds[5], (NTR,), jnp.float32) ** block_scale(seeds[5], (NTR,), ((0, 2),), -0.2, 0.2)), 0.05, 0.5),
        "ocean_indicator": set_ends((jax.random.randint(seeds[6], (MESH_LATITUDES, MESH_LONGITUDES), 0, 10) < 9).astype(jnp.int32), jax.random.fold_in(seeds[6], 1), 0, 1),
        "floor_tier_number": set_ends(jax.random.randint(seeds[7], (MESH_LATITUDES, MESH_LONGITUDES), 1, VERTICAL_TIERS + 1), jax.random.fold_in(seeds[7], 1), 1, VERTICAL_TIERS).astype(jnp.int32),
    }


viscosity = 0.2
water_absorb = 0.04
plankton_absorb = 0.03
heat_share = 0.5
light_half = 0.3
nutrient_half = 0.5


def to_east(values):
    return jnp.concatenate([values[..., 1:], jnp.zeros_like(values[..., :1])], -1)


def to_west(values):
    return jnp.concatenate([jnp.zeros_like(values[..., :1]), values[..., :-1]], -1)


def to_north(values):
    return jnp.concatenate([values[..., 1:, :], jnp.zeros_like(values[..., :1, :])], -2)


def to_south(values):
    return jnp.concatenate([jnp.zeros_like(values[..., :1, :]), values[..., :-1, :]], -2)


def laplace_of(values):
    return to_east(values) + to_west(values) + to_north(values) + to_south(values) - 4.0 * values


def minmod(former, latter):
    return 0.5 * (jnp.sign(former) + jnp.sign(latter)) * jnp.minimum(jnp.abs(former), jnp.abs(latter))


def limited(behind, center, ahead_one, beyond, velocity):
    slope_mid = ahead_one - center
    forward = velocity * (center + 0.5 * (1.0 - velocity) * minmod(slope_mid, center - behind))
    backward = velocity * (ahead_one - 0.5 * (1.0 + velocity) * minmod(slope_mid, beyond - ahead_one))
    return jnp.where(velocity >= 0.0, forward, backward)


def advect_padded(padded, east_pad, north_pad):
    water_span_tiers = padded.shape[-2] - 4
    width_cells = padded.shape[-1] - 4
    row_band = padded[..., 2:water_span_tiers + 2, :]
    flux_x = limited(row_band[..., 0:width_cells + 1], row_band[..., 1:width_cells + 2],
                     row_band[..., 2:width_cells + 3], row_band[..., 3:width_cells + 4],
                     east_pad[:, 2:water_span_tiers + 2, 1:width_cells + 2])
    col_band = padded[..., 2:width_cells + 2]
    flux_y = limited(col_band[..., 0:water_span_tiers + 1, :], col_band[..., 1:water_span_tiers + 2, :],
                     col_band[..., 2:water_span_tiers + 3, :], col_band[..., 3:water_span_tiers + 4, :],
                     north_pad[:, 1:water_span_tiers + 2, 2:width_cells + 2])
    inner_cells = padded[..., 2:water_span_tiers + 2, 2:width_cells + 2]
    return inner_cells - (flux_x[..., 1:] - flux_x[..., :-1]) - (flux_y[..., 1:, :] - flux_y[..., :-1, :])


def vertical_mix(tracer_field, coupling):
    level_below = jnp.concatenate([tracer_field[:, 1:], jnp.zeros_like(tracer_field[:, :1])], 1)
    level_above = jnp.concatenate([jnp.zeros_like(tracer_field[:, :1]), tracer_field[:, :-1]], 1)
    coupling_above = jnp.concatenate([jnp.zeros_like(coupling[:1]), coupling[:-1]], 0)
    return tracer_field + coupling * (level_below - tracer_field) - coupling_above * (tracer_field - level_above)


def light_fields(absorb, solar_flux_field):
    attenuation = water_absorb + plankton_absorb * absorb
    depth_top = jnp.cumsum(attenuation, 0) - attenuation
    light_mid = solar_flux_field * jnp.exp(-depth_top - 0.5 * attenuation)
    heating = heat_share * solar_flux_field * (jnp.exp(-depth_top) - jnp.exp(-depth_top - attenuation))
    return light_mid, heating


def biology(tracer_field, light_mid, rate_values, wet_full):
    tracer_count = tracer_field.shape[0]
    triples = tracer_field.reshape((tracer_count // 3, 3) + tracer_field.shape[1:])
    rate_sets = rate_values.reshape(tracer_count // 3, 3)
    nutrient, plankton, detritus = triples[:, 0], triples[:, 1], triples[:, 2]
    growth = rate_sets[:, 0][:, None, None, None]
    mortal = rate_sets[:, 1][:, None, None, None]
    recycle_rate = rate_sets[:, 2][:, None, None, None]
    uptake = growth * (light_mid / (light_mid + light_half)) * plankton * nutrient / (jnp.abs(nutrient) + nutrient_half)
    mortality = mortal * plankton
    recycled = recycle_rate * detritus
    result = jnp.stack([nutrient - uptake + recycled, plankton + uptake - mortality, detritus + mortality - recycled], 1)
    return result.reshape(tracer_field.shape) * wet_full


def reference(biology_concentration, flow_vectors, thermal_anomaly, diffusivity_profile, solar_flux_field, ecosystem_coefficients, ocean_indicator, floor_tier_number):
    depth_index = jnp.arange(VERTICAL_TIERS, dtype=jnp.int32)[:, None, None]
    wet_full = (ocean_indicator[None] * (depth_index < floor_tier_number[None]).astype(jnp.int32)).astype(jnp.float32)
    open_east = wet_full * to_east(wet_full)
    open_north = wet_full * to_north(wet_full)
    coriolis = (0.1 + 0.1 * jnp.arange(MESH_LATITUDES, dtype=jnp.float32) / MESH_LATITUDES)[:, None]
    wet_below = jnp.concatenate([wet_full[1:], jnp.zeros_like(wet_full[:1])], 0)
    coupling = diffusivity_profile * wet_full * wet_below
    tracer_field = biology_concentration
    east_flow = flow_vectors[0]
    north_flow = flow_vectors[1]
    warming_forcing = thermal_anomaly
    padding = ((0, 0), (0, 0), (2, 2), (2, 2))
    for repeat in range(STEPS):
        east_flux = open_east * east_flow
        north_flux = open_north * north_flow
        next_east = open_east * (east_flow + coriolis * north_flow + viscosity * laplace_of(east_flow))
        next_north = open_north * (north_flow - coriolis * east_flow + viscosity * laplace_of(north_flow))
        padded = jnp.pad(tracer_field, padding)
        east_pad = jnp.pad(east_flux, padding[1:])
        north_pad = jnp.pad(north_flux, padding[1:])
        tracer_field = advect_padded(padded, east_pad, north_pad) * wet_full
        tracer_field = vertical_mix(tracer_field, coupling)
        absorb = jnp.sum(tracer_field[1::3], 0)
        light_mid, heating = light_fields(absorb, solar_flux_field)
        tracer_field = biology(tracer_field, light_mid, ecosystem_coefficients, wet_full)
        eastward = jnp.maximum(east_flux, 0.0) * warming_forcing + jnp.minimum(east_flux, 0.0) * to_east(warming_forcing)
        northward = jnp.maximum(north_flux, 0.0) * warming_forcing + jnp.minimum(north_flux, 0.0) * to_north(warming_forcing)
        warming_forcing = wet_full * (warming_forcing - eastward + to_west(eastward) - northward + to_south(northward) + heating)
        east_flow, north_flow = next_east, next_north
    return tracer_field, jnp.stack([east_flow, north_flow]), warming_forcing
```

```python
import functools

import jax
import jax.numpy as jnp
from jax import lax
from jax.experimental import pallas as pl
from jax.experimental.pallas import tpu as pltpu
from jax.sharding import PartitionSpec as P

STEPS = 2
viscosity = 0.2
water_absorb = 0.04
plankton_absorb = 0.03
heat_share = 0.5
light_half = 0.3
nutrient_half = 0.5
SLOTS = 32
F32 = jnp.float32


def minmod(a, b):
    return jnp.maximum(jnp.minimum(a, b), jnp.minimum(jnp.maximum(a, b), 0.0))


def kernel(nx, ny, nt, NT, LV, LO, H, W,
           c_ref, flow_ref, temp_ref, kv_ref, sol_ref, eco_ref, ocean_ref, floor_ref,
           out_ref, outf_ref, outt_ref,
           cp1, cp2, xp1, xp2, xe1, xe2, xw1, xw2, hc, hs,
           flow_all, temp_all, flow_out, coef, sy, part, arecv,
           fs, fr, hsend, hrecv, asend, arec_sem):
    gx, gy, t = lax.axis_index("gx"), lax.axis_index("gy"), lax.axis_index("tracer")
    WET, TF, UF, VF = 0, NT + 1, NT + 2, NT + 3
    G = H // SLOTS
    NCH = asend.shape[1]
    CH = H // NCH
    own = pl.multiple_of(t * (LO * H), 8)
    lane = lax.broadcasted_iota(jnp.int32, (LV, W), 1)
    level = lax.broadcasted_iota(jnp.int32, (LV, W), 0)
    lane_slot = lane // 4
    first, last = lane == 0, lane == W - 1
    half = (lane % 4) < 2
    sgn = jnp.where(half, 1.0, -1.0).astype(F32)

    has = (gy < ny - 1, gy > 0, gx < nx - 1, gx > 0)
    came = (gy > 0, gy < ny - 1, gx > 0, gx < nx - 1)
    peer = ({"gy": lax.rem(gy + 1, ny)}, {"gy": lax.rem(gy + ny - 1, ny)},
            {"gx": lax.rem(gx + 1, nx)}, {"gx": lax.rem(gx + nx - 1, nx)})
    barrier = pltpu.get_barrier_semaphore()
    for d in range(4):
        @pl.when(has[d])
        def _():
            pl.semaphore_signal(barrier, inc=1, device_id=peer[d], device_id_type=pl.DeviceIdType.MESH)
    for d in range(1, nt):
        pl.semaphore_signal(barrier, inc=1, device_id={"tracer": lax.rem(t + d, nt)},
                            device_id_type=pl.DeviceIdType.MESH)
    pl.semaphore_wait(barrier, sum(x.astype(jnp.int32) for x in has) + (nt - 1))

    def remote(src, dst, ss, rs, dev):
        return pltpu.make_async_remote_copy(src_ref=src, dst_ref=dst, send_sem=ss, recv_sem=rs,
                                            device_id=dev, device_id_type=pl.DeviceIdType.MESH)

    flows = [remote(flow_ref, flow_all.at[:, pl.ds(own, LO * H), :], fs.at[d], fr.at[d],
                    {"tracer": lax.rem(t + d, nt)}) for d in range(1, nt)]
    for cp in flows:
        cp.start()

    def exchange(step, grp, cp, xp, xe, xw, lo, n):
        f = pl.ds(lo, n)
        pairs = ((cp.at[f, pl.ds(H, 2)], cp.at[f, pl.ds(0, 2)]),
                 (cp.at[f, pl.ds(2, 2)], cp.at[f, pl.ds(H + 2, 2)]),
                 (xp.at[f], xw.at[f]), (xp.at[f], xe.at[f]))
        return [remote(s, r, hsend.at[step, grp, d], hrecv.at[step, grp, d], peer[d])
                for d, (s, r) in enumerate(pairs)]

    def start(copies, dirs):
        for d in dirs:
            @pl.when(has[d])
            def _():
                copies[d].start()

    def wait_recv(copies):
        for d in range(4):
            @pl.when(came[d])
            def _():
                copies[d].wait_recv()

    def wait_send(copies):
        for d in range(4):
            @pl.when(has[d])
            def _():
                copies[d].wait_send()

    def pack(cp, xp, lo, n):
        def body(f, _):
            for g in range(G):
                acc = jnp.zeros((LV, W), F32)
                for j in range(SLOTS):
                    row = cp[f, 2 + g * SLOTS + j]
                    acc = jnp.where(lane_slot == j, pltpu.roll(row, (4 * j + 2) % W, 1), acc)
                xp[f, g] = acc
            return 0
        lax.fori_loop(lo, lo + n, body, 0)

    def unpack(xp, xe, xw, lo, n):
        def body(f, _):
            for g in range(G):
                o, e, w = xp[f, g], xe[f, g], xw[f, g]
                near = jnp.where(half, pltpu.roll(e, W - 1, 1), pltpu.roll(w, 1, 1))
                far = jnp.where(half, pltpu.roll(e, W - 2, 1), pltpu.roll(w, 2, 1))
                hc[f, g] = near
                hs[f, g] = sgn * minmod(far - near, near - o)
            return 0
        lax.fori_loop(lo, lo + n, body, 0)

    def clear_edges(cp, xe, xw):
        NF = NT + 4
        zrow = jnp.zeros((NF, 2, LV, W), F32)
        zx = jnp.zeros((NF, G, LV, W), F32)
        @pl.when(gy == 0)
        def _():
            cp[:, 0:2] = zrow
        @pl.when(gy == ny - 1)
        def _():
            cp[:, H + 2:H + 4] = zrow
        @pl.when(gx == nx - 1)
        def _():
            xe[...] = zx
        @pl.when(gx == 0)
        def _():
            xw[...] = zx

    def rows(ref, y):
        return ref[pl.ds(y, LV, stride=H), :]

    temp_all[...] = jnp.zeros((LV * H, W), F32)
    temp_all[pl.ds(own, LO * H), :] = temp_ref[...]
    flow_all[:, pl.ds(own, LO * H), :] = flow_ref[...]
    clear_edges(cp1, xe1, xw1)
    clear_edges(cp2, xe2, xw2)

    def load(y, _):
        depth = ocean_ref[pl.ds(y, 1), :] * floor_ref[pl.ds(y, 1), :]
        cp1[WET, y + 2] = jnp.where(level < jnp.broadcast_to(depth, (LV, W)), 1.0, 0.0).astype(F32)
        for k in range(NT):
            cp1[1 + k, y + 2] = rows(c_ref.at[k], y)
        cp1[TF, y + 2] = rows(temp_all, y)
        return 0
    lax.fori_loop(0, H, load, 0)

    a1 = exchange(0, 0, cp1, xp1, xe1, xw1, 0, NT + 2)
    b1 = exchange(0, 1, cp1, xp1, xe1, xw1, UF, 2)
    a2 = exchange(1, 0, cp2, xp2, xe2, xw2, 1, NT + 1)
    b2 = exchange(1, 1, cp2, xp2, xe2, xw2, UF, 2)
    start(a1, (0, 1))
    pack(cp1, xp1, 0, NT + 2)
    start(a1, (2, 3))

    for cp in flows:
        cp.wait_recv()

    def load_flow(y, _):
        cp1[UF, y + 2] = rows(flow_all.at[0], y)
        cp1[VF, y + 2] = rows(flow_all.at[1], y)
        return 0
    lax.fori_loop(0, H, load_flow, 0)
    start(b1, (0, 1))
    pack(cp1, xp1, UF, 2)
    start(b1, (2, 3))
    wait_recv(a1)
    unpack(xp1, xe1, xw1, 0, NT + 2)
    wait_recv(b1)
    unpack(xp1, xe1, xw1, UF, 2)

    grid_rows = H * ny

    def halo(ref, f, y):
        return pltpu.roll(ref[f, y // SLOTS], W - 2 - 4 * lax.rem(y, SLOTS), 1)

    def sides(q, h):
        return (jnp.where(last, h, pltpu.roll(q, W - 1, 1)), jnp.where(first, h, pltpu.roll(q, 1, 1)))

    def currents(cp, store):
        def body(y, _):
            wet, wn, ws = cp1[WET, y + 2], cp1[WET, y + 3], cp1[WET, y + 1]
            u, un, us = cp[UF, y + 2], cp[UF, y + 3], cp[UF, y + 1]
            v, vn, vs = cp[VF, y + 2], cp[VF, y + 3], cp[VF, y + 1]
            we = coef[14, y]
            ww = coef[15, y]
            ue, uw = sides(u, halo(hc, UF, y))
            ve, vw = sides(v, halo(hc, VF, y))
            oe, on = wet * we, wet * wn
            cor = 0.1 + 0.1 * (gy * H + y).astype(F32) / grid_rows
            lap_u = ue + uw + un + us - 4.0 * u
            lap_v = ve + vw + vn + vs - 4.0 * v
            store(y, oe * (u + cor * v + viscosity * lap_u), on * (v - cor * u + viscosity * lap_v))
            U, V = oe * u, on * v
            Uw, Vs = wet * ww * uw, wet * ws * vs
            pe, me, pw, mw = jnp.maximum(U, 0.0), jnp.minimum(U, 0.0), jnp.maximum(Uw, 0.0), jnp.minimum(Uw, 0.0)
            pn, mn, ps, ms = jnp.maximum(V, 0.0), jnp.minimum(V, 0.0), jnp.maximum(Vs, 0.0), jnp.minimum(Vs, 0.0)
            coef[0, y] = wet * (1.0 - pe + mw - pn + ms)
            coef[1, y] = -(wet * me)
            coef[2, y] = wet * pw
            coef[3, y] = -0.5 * wet * (pe * (1.0 - U) + mw * (1.0 + Uw))
            coef[4, y] = 0.5 * wet * me * (1.0 + U)
            coef[5, y] = 0.5 * wet * pw * (1.0 - Uw)
            coef[6, y] = -(wet * mn)
            coef[7, y] = wet * ps
            coef[8, y] = -0.5 * wet * (pn * (1.0 - V) + ms * (1.0 + Vs))
            coef[9, y] = 0.5 * wet * mn * (1.0 + V)
            coef[10, y] = 0.5 * wet * ps * (1.0 - Vs)
            return 0
        lax.fori_loop(0, H, body, 0)

    def masks(y, _):
        wet = cp1[WET, y + 2]
        we, ww = sides(wet, halo(hc, WET, y))
        coef[14, y] = we
        coef[15, y] = ww
        below = jnp.where(level < LV - 1, pltpu.roll(wet, LV - 1, 0), 0.0)
        kv = rows(kv_ref, y) * wet * below
        up = pltpu.roll(kv, 1, 0)
        coef[11, y] = 1.0 - kv - up
        coef[12, y] = kv
        coef[13, y] = up
        return 0
    lax.fori_loop(0, H, masks, 0)

    def slopes_first(cp):
        for f in range(1, NT + 1):
            c = [cp[f, i] for i in range(4)]
            sy[f - 1, 0] = minmod(c[2] - c[1], c[1] - c[0])
            sy[f - 1, 1] = minmod(c[3] - c[2], c[2] - c[1])

    def advect(cp, f, y, co):
        c, cs, cn, cnn = cp[f, y + 2], cp[f, y + 1], cp[f, y + 3], cp[f, y + 4]
        sn = minmod(cnn - cn, cn - c)
        s0, ss = sy[f - 1, y + 1], sy[f - 1, y]
        sy[f - 1, y + 2] = sn
        ce, cw = sides(c, halo(hc, f, y))
        sx = minmod(ce - c, c - cw)
        se, sw = sides(sx, halo(hs, f, y))
        adv = ((co[0] * c + co[1] * ce) + (co[2] * cw + co[3] * sx)) + ((co[4] * se + co[5] * sw) + (
            co[6] * cn + co[7] * cs)) + ((co[8] * s0 + co[9] * sn) + co[10] * ss)
        return co[11] * adv + (co[12] * pltpu.roll(adv, LV - 1, 0) + co[13] * pltpu.roll(adv, 1, 0))

    def tracers(cp, dst, step):
        slopes_first(cp)
        sends = [[remote(part.at[step, pl.ds(q * CH, CH)], arecv.at[step, d - 1, pl.ds(q * CH, CH)],
                         asend.at[step, q, d], arec_sem.at[step, q, d],
                         {"tracer": lax.rem(t + d, nt)}) for d in range(1, nt)] for q in range(NCH)]

        def plankton(y, _):
            co = [coef[i, y] for i in range(14)]
            total = None
            for k in range(1, NT, 3):
                m = advect(cp, 1 + k, y, co)
                dst[1 + k, y + 2] = m
                total = m if total is None else total + m
            part[step, y] = total
            return 0

        def others(y, _):
            co = [coef[i, y] for i in range(14)]
            for k in range(NT):
                if k % 3 != 1:
                    dst[1 + k, y + 2] = advect(cp, 1 + k, y, co)
            return 0
        for q in range(NCH):
            lax.fori_loop(q * CH, (q + 1) * CH, plankton, 0)
            for cp_ in sends[q]:
                cp_.start()
        lax.fori_loop(0, H, others, 0)
        return sends

    def ecology(cp, mix, step, sends, put, put_temp):
        rate = [eco_ref[k] for k in range(NT)]

        def body(y, _):
            total = part[step, y]
            for d in range(nt - 1):
                total = total + arecv[step, d, y]
            a = water_absorb + plankton_absorb * total
            acc = a
            for sh in (1, 2, 4):
                if sh < LV:
                    acc = acc + jnp.where(level >= sh, pltpu.roll(acc, sh, 0), 0.0)
            tau = acc - a
            sol = jnp.broadcast_to(sol_ref[pl.ds(y, 1), :], (LV, W))
            light = sol * jnp.exp(-tau - 0.5 * a)
            heat = heat_share * sol * (jnp.exp(-tau) - jnp.exp(-tau - a))
            lim = light / (light + light_half)
            wet = cp1[WET, y + 2]
            for k in range(0, NT, 3):
                n, p, dt = mix[1 + k, y + 2], mix[2 + k, y + 2], mix[3 + k, y + 2]
                uptake = (rate[k] * lim) * p * n / (jnp.abs(n) + nutrient_half)
                dead, back = rate[k + 1] * p, rate[k + 2] * dt
                put(k, y, wet * (n - uptake + back))
                put(k + 1, y, wet * (p + uptake - dead))
                put(k + 2, y, wet * (dt + dead - back))
            tm = cp[TF, y + 2]
            te, tw = sides(tm, halo(hc, TF, y))
            put_temp(y, coef[0, y] * tm + coef[1, y] * te + coef[2, y] * tw
                     + coef[6, y] * cp[TF, y + 3] + coef[7, y] * cp[TF, y + 1] + wet * heat)
            return 0
        for q in range(NCH):
            for cp_ in sends[q]:
                cp_.wait_recv()
            lax.fori_loop(q * CH, (q + 1) * CH, body, 0)
        for q in range(NCH):
            for cp_ in sends[q]:
                cp_.wait_send()

    def store_next(y, u, v):
        cp2[UF, y + 2] = u
        cp2[VF, y + 2] = v
    currents(cp1, store_next)
    start(b2, (0, 1))
    pack(cp2, xp2, UF, 2)
    start(b2, (2, 3))
    sends = tracers(cp1, cp2, 0)

    def put_next(k, y, value):
        cp2[1 + k, y + 2] = value

    def put_temp_next(y, value):
        cp2[TF, y + 2] = value
    ecology(cp1, cp2, 0, sends, put_next, put_temp_next)
    start(a2, (0, 1))
    pack(cp2, xp2, 1, NT + 1)
    start(a2, (2, 3))

    wait_recv(b2)
    unpack(xp2, xe2, xw2, UF, 2)

    def store_last(y, u, v):
        flow_out[0, pl.ds(y, LV, stride=H), :] = u
        flow_out[1, pl.ds(y, LV, stride=H), :] = v
    currents(cp2, store_last)
    outf_ref[...] = flow_out[:, pl.ds(own, LO * H), :]
    wait_send(a1)
    wait_send(b1)
    for cp in flows:
        cp.wait_send()
    wait_recv(a2)
    unpack(xp2, xe2, xw2, 1, NT + 1)
    sends = tracers(cp2, cp1, 1)

    def put_last(k, y, value):
        out_ref[k, pl.ds(y, LV, stride=H), :] = value

    def put_temp_last(y, value):
        temp_all[pl.ds(y, LV, stride=H), :] = value
    ecology(cp2, cp1, 1, sends, put_last, put_temp_last)
    outt_ref[...] = temp_all[pl.ds(own, LO * H), :]
    wait_send(a2)
    wait_send(b2)


def per_device(nx, ny, nt, c, flow, temp, kv, sol, eco, ocean, floor):
    NT, LV, H, W = c.shape
    LO = temp.shape[0]
    NF, G = NT + 4, H // SLOTS
    assert H % SLOTS == 0 and W == 4 * SLOTS
    NCH = 4
    vm = pltpu.VMEM
    dma = pltpu.SemaphoreType.DMA
    field = vm((NF, H + 4, LV, W), F32)
    edge = vm((NF, G, LV, W), F32)
    whole = pl.BlockSpec(memory_space=pltpu.VMEM)
    out, outf, outt = pl.pallas_call(
        functools.partial(kernel, nx, ny, nt, NT, LV, LO, H, W),
        out_shape=(jax.ShapeDtypeStruct((NT, LV * H, W), F32),
                   jax.ShapeDtypeStruct((2, LO * H, W), F32),
                   jax.ShapeDtypeStruct((LO * H, W), F32)),
        in_specs=[whole] * 5 + [pl.BlockSpec(memory_space=pltpu.SMEM)] + [whole] * 2,
        out_specs=(whole,) * 3,
        scratch_shapes=[field, field, edge, edge, edge, edge, edge, edge, edge, edge,
                        vm((2, LV * H, W), F32), vm((LV * H, W), F32), vm((2, LV * H, W), F32),
                        vm((16, H, LV, W), F32), vm((NT, H + 2, LV, W), F32),
                        vm((STEPS, H, LV, W), F32), vm((STEPS, max(nt - 1, 1), H, LV, W), F32),
                        dma((nt,)), dma((nt,)), dma((STEPS, 2, 4)), dma((STEPS, 2, 4)),
                        dma((STEPS, NCH, nt)), dma((STEPS, NCH, nt))],
        compiler_params=pltpu.CompilerParams(collective_id=0, has_side_effects=True,
                                             vmem_limit_bytes=60 * 1024 * 1024),
        name="ocean",
    )(c.reshape(NT, LV * H, W), flow.reshape(2, LO * H, W), temp.reshape(LO * H, W),
      kv.reshape(LV * H, W), sol, eco, ocean, floor)
    return out.reshape(c.shape), outf.reshape(flow.shape), outt.reshape(temp.shape)


def solution(mesh):
    in_specs = (
        P("tracer", None, "gy", "gx"),
        P(None, "tracer", "gy", "gx"),
        P("tracer", "gy", "gx"),
        P(None, "gy", "gx"),
        P("gy", "gx"),
        P("tracer"),
        P("gy", "gx"),
        P("gy", "gx"),
    )
    out_specs = (
        P("tracer", None, "gy", "gx"),
        P(None, "tracer", "gy", "gx"),
        P("tracer", "gy", "gx"),
    )
    body = functools.partial(per_device, mesh.shape["gx"], mesh.shape["gy"], mesh.shape["tracer"])
    return jax.shard_map(body, mesh=mesh, in_specs=in_specs, out_specs=out_specs, check_vma=False)
```

```python
import functools

import jax
import jax.numpy as jnp
from jax import lax
from jax.experimental import pallas as pl
from jax.experimental.pallas import tpu as pltpu
from jax.sharding import PartitionSpec as P

STEPS = 2
viscosity = 0.2
water_absorb = 0.04
plankton_absorb = 0.03
heat_share = 0.5
light_half = 0.3
nutrient_half = 0.5
SLOTS = 32
ROWS = 8
F32 = jnp.float32


def minmod(a, b):
    return jnp.maximum(jnp.minimum(a, b), jnp.minimum(jnp.maximum(a, b), 0.0))


def kernel(nx, ny, nt, NT, LV, LO, H, W,
           c_ref, flow_ref, temp_ref, kv_ref, sol_ref, eco_ref, ocean_ref, floor_ref,
           out_ref, outf_ref, outt_ref,
           cp1, cp2, xp1, xp2, xe1, xe2, xw1, xw2, hc, hs,
           flow_all, temp_all, flow_out, coef, part, arecv,
           fs, fr, hsend, hrecv, asend, arec_sem):
    gx, gy, t = lax.axis_index("gx"), lax.axis_index("gy"), lax.axis_index("tracer")
    WET, TF, UF, VF = 0, NT + 1, NT + 2, NT + 3
    G = H // SLOTS
    NCH = asend.shape[1]
    CH = H // NCH
    own = pl.multiple_of(t * (LO * H), 8)
    lane = lax.broadcasted_iota(jnp.int32, (LV, W), 1)
    level = lax.broadcasted_iota(jnp.int32, (LV, W), 0)
    lane_slot = lane // 4
    first, last = lane == 0, lane == W - 1
    half = (lane % 4) < 2
    sgn = jnp.where(half, 1.0, -1.0).astype(F32)

    has = (gy < ny - 1, gy > 0, gx < nx - 1, gx > 0)
    came = (gy > 0, gy < ny - 1, gx > 0, gx < nx - 1)
    peer = ({"gy": lax.rem(gy + 1, ny)}, {"gy": lax.rem(gy + ny - 1, ny)},
            {"gx": lax.rem(gx + 1, nx)}, {"gx": lax.rem(gx + nx - 1, nx)})
    barrier = pltpu.get_barrier_semaphore()
    for d in range(4):
        @pl.when(has[d])
        def _():
            pl.semaphore_signal(barrier, inc=1, device_id=peer[d], device_id_type=pl.DeviceIdType.MESH)
    for d in range(1, nt):
        pl.semaphore_signal(barrier, inc=1, device_id={"tracer": lax.rem(t + d, nt)},
                            device_id_type=pl.DeviceIdType.MESH)
    pl.semaphore_wait(barrier, sum(x.astype(jnp.int32) for x in has) + (nt - 1))

    def remote(src, dst, ss, rs, dev):
        return pltpu.make_async_remote_copy(src_ref=src, dst_ref=dst, send_sem=ss, recv_sem=rs,
                                            device_id=dev, device_id_type=pl.DeviceIdType.MESH)

    flows = [remote(flow_ref, flow_all.at[:, pl.ds(own, LO * H), :], fs.at[d], fr.at[d],
                    {"tracer": lax.rem(t + d, nt)}) for d in range(1, nt)]
    for cp in flows:
        cp.start()

    def exchange(step, grp, cp, xp, xe, xw, lo, n):
        f = pl.ds(lo, n)
        pairs = ((cp.at[f, pl.ds(H, 2)], cp.at[f, pl.ds(0, 2)]),
                 (cp.at[f, pl.ds(2, 2)], cp.at[f, pl.ds(H + 2, 2)]),
                 (xp.at[f], xw.at[f]), (xp.at[f], xe.at[f]))
        return [remote(s, r, hsend.at[step, grp, d], hrecv.at[step, grp, d], peer[d])
                for d, (s, r) in enumerate(pairs)]

    def start(copies, dirs):
        for d in dirs:
            @pl.when(has[d])
            def _():
                copies[d].start()

    def wait_recv(copies):
        for d in range(4):
            @pl.when(came[d])
            def _():
                copies[d].wait_recv()

    def wait_send(copies):
        for d in range(4):
            @pl.when(has[d])
            def _():
                copies[d].wait_send()

    def pack(cp, xp, lo, n):
        def body(f, _):
            for g in range(G):
                acc = jnp.zeros((LV, W), F32)
                for j in range(SLOTS):
                    row = cp[f, 2 + g * SLOTS + j]
                    acc = jnp.where(lane_slot == j, pltpu.roll(row, (4 * j + 2) % W, 1), acc)
                xp[f, g] = acc
            return 0
        lax.fori_loop(lo, lo + n, body, 0)

    def unpack(xp, xe, xw, lo, n):
        def body(f, _):
            for g in range(G):
                o, e, w = xp[f, g], xe[f, g], xw[f, g]
                near = jnp.where(half, pltpu.roll(e, W - 1, 1), pltpu.roll(w, 1, 1))
                far = jnp.where(half, pltpu.roll(e, W - 2, 1), pltpu.roll(w, 2, 1))
                hc[f, g] = near
                hs[f, g] = sgn * minmod(far - near, near - o)
            return 0
        lax.fori_loop(lo, lo + n, body, 0)

    def clear_edges(cp, xe, xw):
        NF = NT + 4
        zrow = jnp.zeros((NF, 2, LV, W), F32)
        zx = jnp.zeros((NF, G, LV, W), F32)
        @pl.when(gy == 0)
        def _():
            cp[:, 0:2] = zrow
        @pl.when(gy == ny - 1)
        def _():
            cp[:, H + 2:H + 4] = zrow
        @pl.when(gx == nx - 1)
        def _():
            xe[...] = zx
        @pl.when(gx == 0)
        def _():
            xw[...] = zx

    def each_row(lo, hi, n, fn):
        def body(i, _):
            for r in range(n):
                fn(i * n + r, 0)
            return 0
        lax.fori_loop(lo // n, hi // n, body, 0)

    def rows(ref, y):
        return ref[pl.ds(y, LV, stride=H), :]

    temp_all[...] = jnp.zeros((LV * H, W), F32)
    temp_all[pl.ds(own, LO * H), :] = temp_ref[...]
    flow_all[:, pl.ds(own, LO * H), :] = flow_ref[...]
    clear_edges(cp1, xe1, xw1)
    clear_edges(cp2, xe2, xw2)

    def load(y, _):
        depth = ocean_ref[pl.ds(y, 1), :] * floor_ref[pl.ds(y, 1), :]
        cp1[WET, y + 2] = jnp.where(level < jnp.broadcast_to(depth, (LV, W)), 1.0, 0.0).astype(F32)
        for k in range(NT):
            cp1[1 + k, y + 2] = rows(c_ref.at[k], y)
        cp1[TF, y + 2] = rows(temp_all, y)
        return 0
    each_row(0, H, 2, load)

    a1 = exchange(0, 0, cp1, xp1, xe1, xw1, 0, NT + 2)
    b1 = exchange(0, 1, cp1, xp1, xe1, xw1, UF, 2)
    a2 = exchange(1, 0, cp2, xp2, xe2, xw2, 1, NT + 1)
    b2 = exchange(1, 1, cp2, xp2, xe2, xw2, UF, 2)
    start(a1, (0, 1))
    pack(cp1, xp1, 0, NT + 2)
    start(a1, (2, 3))

    for cp in flows:
        cp.wait_recv()

    def load_flow(y, _):
        cp1[UF, y + 2] = rows(flow_all.at[0], y)
        cp1[VF, y + 2] = rows(flow_all.at[1], y)
        return 0
    each_row(0, H, 8, load_flow)
    start(b1, (0, 1))
    pack(cp1, xp1, UF, 2)
    start(b1, (2, 3))
    wait_recv(a1)
    unpack(xp1, xe1, xw1, 0, NT + 2)
    wait_recv(b1)
    unpack(xp1, xe1, xw1, UF, 2)

    grid_rows = H * ny

    def halo(ref, f, y):
        return pltpu.roll(ref[f, y // SLOTS], W - 2 - 4 * lax.rem(y, SLOTS), 1)

    def sides(q, h):
        return (jnp.where(last, h, pltpu.roll(q, W - 1, 1)), jnp.where(first, h, pltpu.roll(q, 1, 1)))

    def currents(cp, store):
        def body(y, _):
            wet, wn, ws = cp1[WET, y + 2], cp1[WET, y + 3], cp1[WET, y + 1]
            u, un, us = cp[UF, y + 2], cp[UF, y + 3], cp[UF, y + 1]
            v, vn, vs = cp[VF, y + 2], cp[VF, y + 3], cp[VF, y + 1]
            we = coef[14, y]
            ww = coef[15, y]
            ue, uw = sides(u, halo(hc, UF, y))
            ve, vw = sides(v, halo(hc, VF, y))
            oe, on = wet * we, wet * wn
            cor = 0.1 + 0.1 * (gy * H + y).astype(F32) / grid_rows
            lap_u = ue + uw + un + us - 4.0 * u
            lap_v = ve + vw + vn + vs - 4.0 * v
            store(y, oe * (u + cor * v + viscosity * lap_u), on * (v - cor * u + viscosity * lap_v))
            U, V = oe * u, on * v
            Uw, Vs = wet * ww * uw, wet * ws * vs
            pe, me, pw, mw = jnp.maximum(U, 0.0), jnp.minimum(U, 0.0), jnp.maximum(Uw, 0.0), jnp.minimum(Uw, 0.0)
            pn, mn, ps, ms = jnp.maximum(V, 0.0), jnp.minimum(V, 0.0), jnp.maximum(Vs, 0.0), jnp.minimum(Vs, 0.0)
            coef[0, y] = wet * (1.0 - pe + mw - pn + ms)
            coef[1, y] = -(wet * me)
            coef[2, y] = wet * pw
            coef[3, y] = -0.5 * wet * (pe * (1.0 - U) + mw * (1.0 + Uw))
            coef[4, y] = 0.5 * wet * me * (1.0 + U)
            coef[5, y] = 0.5 * wet * pw * (1.0 - Uw)
            coef[6, y] = -(wet * mn)
            coef[7, y] = wet * ps
            coef[8, y] = -0.5 * wet * (pn * (1.0 - V) + ms * (1.0 + Vs))
            coef[9, y] = 0.5 * wet * mn * (1.0 + V)
            coef[10, y] = 0.5 * wet * ps * (1.0 - Vs)
            return 0
        each_row(0, H, 4, body)

    def masks(y, _):
        wet = cp1[WET, y + 2]
        we, ww = sides(wet, halo(hc, WET, y))
        coef[14, y] = we
        coef[15, y] = ww
        below = jnp.where(level < LV - 1, pltpu.roll(wet, LV - 1, 0), 0.0)
        kv = rows(kv_ref, y) * wet * below
        up = pltpu.roll(kv, 1, 0)
        coef[11, y] = 1.0 - kv - up
        coef[12, y] = kv
        coef[13, y] = up
        return 0
    each_row(0, H, 8, masks)

    def advect(cp, f, b):
        base = b * ROWS
        c = [cp[f, base + i] for i in range(ROWS + 4)]
        d = [c[i + 1] - c[i] for i in range(ROWS + 3)]
        s = [minmod(d[i + 1], d[i]) for i in range(ROWS + 2)]
        group = base // SLOTS
        near, slope = hc[f, group], hs[f, group]
        turn = W - 2 - 4 * lax.rem(base, SLOTS)
        out = []
        for r in range(ROWS):
            y = base + r
            m = c[r + 2]
            ce, cw = sides(m, pltpu.roll(near, turn - 4 * r, 1))
            sx = minmod(ce - m, m - cw)
            se, sw = sides(sx, pltpu.roll(slope, turn - 4 * r, 1))
            x = (coef[0, y] * m + coef[1, y] * ce) + (coef[2, y] * cw + coef[3, y] * sx)
            x = x + (coef[4, y] * se + coef[5, y] * sw)
            z = (coef[6, y] * c[r + 3] + coef[7, y] * c[r + 1]) + (coef[8, y] * s[r + 1] + coef[9, y] * s[r + 2])
            adv = x + (z + coef[10, y] * s[r])
            out.append(coef[11, y] * adv + (coef[12, y] * pltpu.roll(adv, LV - 1, 0)
                                            + coef[13, y] * pltpu.roll(adv, 1, 0)))
        return out

    def tracers(cp, dst, step):
        sends = [[remote(part.at[step, pl.ds(q * CH, CH)], arecv.at[step, d - 1, pl.ds(q * CH, CH)],
                         asend.at[step, q, d], arec_sem.at[step, q, d],
                         {"tracer": lax.rem(t + d, nt)}) for d in range(1, nt)] for q in range(NCH)]

        def plankton(b, _):
            total = None
            for k in range(1, NT, 3):
                m = advect(cp, 1 + k, b)
                for r in range(ROWS):
                    dst[1 + k, b * ROWS + r + 2] = m[r]
                total = m if total is None else [p + q for p, q in zip(total, m)]
            for r in range(ROWS):
                part[step, b * ROWS + r] = total[r]
            return 0

        def others(b, _):
            for k in range(NT):
                if k % 3 != 1:
                    m = advect(cp, 1 + k, b)
                    for r in range(ROWS):
                        dst[1 + k, b * ROWS + r + 2] = m[r]
            return 0
        BC = CH // ROWS
        for q in range(NCH):
            lax.fori_loop(q * BC, (q + 1) * BC, plankton, 0)
            for cp_ in sends[q]:
                cp_.start()
        lax.fori_loop(0, H // ROWS, others, 0)
        return sends

    def ecology(cp, mix, step, sends, put, put_temp):
        rate = [eco_ref[k] for k in range(NT)]

        def body(y, _):
            total = part[step, y]
            for d in range(nt - 1):
                total = total + arecv[step, d, y]
            a = water_absorb + plankton_absorb * total
            acc = a
            for sh in (1, 2, 4):
                if sh < LV:
                    acc = acc + jnp.where(level >= sh, pltpu.roll(acc, sh, 0), 0.0)
            tau = acc - a
            sol = jnp.broadcast_to(sol_ref[pl.ds(y, 1), :], (LV, W))
            light = sol * jnp.exp(-tau - 0.5 * a)
            heat = heat_share * sol * (jnp.exp(-tau) - jnp.exp(-tau - a))
            lim = light / (light + light_half)
            wet = cp1[WET, y + 2]
            for k in range(0, NT, 3):
                n, p, dt = mix[1 + k, y + 2], mix[2 + k, y + 2], mix[3 + k, y + 2]
                uptake = (rate[k] * lim) * p * n / (jnp.abs(n) + nutrient_half)
                dead, back = rate[k + 1] * p, rate[k + 2] * dt
                put(k, y, wet * (n - uptake + back))
                put(k + 1, y, wet * (p + uptake - dead))
                put(k + 2, y, wet * (dt + dead - back))
            tm = cp[TF, y + 2]
            te, tw = sides(tm, halo(hc, TF, y))
            put_temp(y, coef[0, y] * tm + coef[1, y] * te + coef[2, y] * tw
                     + coef[6, y] * cp[TF, y + 3] + coef[7, y] * cp[TF, y + 1] + wet * heat)
            return 0
        for q in range(NCH):
            for cp_ in sends[q]:
                cp_.wait_recv()
            each_row(q * CH, (q + 1) * CH, 4, body)
        for q in range(NCH):
            for cp_ in sends[q]:
                cp_.wait_send()

    def store_next(y, u, v):
        cp2[UF, y + 2] = u
        cp2[VF, y + 2] = v
    currents(cp1, store_next)
    start(b2, (0, 1))
    pack(cp2, xp2, UF, 2)
    start(b2, (2, 3))
    sends = tracers(cp1, cp2, 0)

    def put_next(k, y, value):
        cp2[1 + k, y + 2] = value

    def put_temp_next(y, value):
        cp2[TF, y + 2] = value
    ecology(cp1, cp2, 0, sends, put_next, put_temp_next)
    start(a2, (0, 1))
    pack(cp2, xp2, 1, NT + 1)
    start(a2, (2, 3))

    wait_recv(b2)
    unpack(xp2, xe2, xw2, UF, 2)

    def store_last(y, u, v):
        flow_out[0, pl.ds(y, LV, stride=H), :] = u
        flow_out[1, pl.ds(y, LV, stride=H), :] = v
    currents(cp2, store_last)
    outf_ref[...] = flow_out[:, pl.ds(own, LO * H), :]
    wait_send(a1)
    wait_send(b1)
    for cp in flows:
        cp.wait_send()
    wait_recv(a2)
    unpack(xp2, xe2, xw2, 1, NT + 1)
    sends = tracers(cp2, cp1, 1)

    def put_last(k, y, value):
        out_ref[k, pl.ds(y, LV, stride=H), :] = value

    def put_temp_last(y, value):
        temp_all[pl.ds(y, LV, stride=H), :] = value
    ecology(cp2, cp1, 1, sends, put_last, put_temp_last)
    outt_ref[...] = temp_all[pl.ds(own, LO * H), :]
    wait_send(a2)
    wait_send(b2)


def per_device(nx, ny, nt, c, flow, temp, kv, sol, eco, ocean, floor):
    NT, LV, H, W = c.shape
    LO = temp.shape[0]
    NF, G = NT + 4, H // SLOTS
    assert H % SLOTS == 0 and W == 4 * SLOTS
    NCH = 4
    vm = pltpu.VMEM
    dma = pltpu.SemaphoreType.DMA
    field = vm((NF, H + 4, LV, W), F32)
    edge = vm((NF, G, LV, W), F32)
    whole = pl.BlockSpec(memory_space=pltpu.VMEM)
    out, outf, outt = pl.pallas_call(
        functools.partial(kernel, nx, ny, nt, NT, LV, LO, H, W),
        out_shape=(jax.ShapeDtypeStruct((NT, LV * H, W), F32),
                   jax.ShapeDtypeStruct((2, LO * H, W), F32),
                   jax.ShapeDtypeStruct((LO * H, W), F32)),
        in_specs=[whole] * 5 + [pl.BlockSpec(memory_space=pltpu.SMEM)] + [whole] * 2,
        out_specs=(whole,) * 3,
        scratch_shapes=[field, field, edge, edge, edge, edge, edge, edge, edge, edge,
                        vm((2, LV * H, W), F32), vm((LV * H, W), F32), vm((2, LV * H, W), F32),
                        vm((16, H, LV, W), F32),
                        vm((STEPS, H, LV, W), F32), vm((STEPS, max(nt - 1, 1), H, LV, W), F32),
                        dma((nt,)), dma((nt,)), dma((STEPS, 2, 4)), dma((STEPS, 2, 4)),
                        dma((STEPS, NCH, nt)), dma((STEPS, NCH, nt))],
        compiler_params=pltpu.CompilerParams(collective_id=0, has_side_effects=True,
                                             vmem_limit_bytes=60 * 1024 * 1024),
        name="ocean",
    )(c.reshape(NT, LV * H, W), flow.reshape(2, LO * H, W), temp.reshape(LO * H, W),
      kv.reshape(LV * H, W), sol, eco, ocean, floor)
    return out.reshape(c.shape), outf.reshape(flow.shape), outt.reshape(temp.shape)


def solution(mesh):
    in_specs = (
        P("tracer", None, "gy", "gx"),
        P(None, "tracer", "gy", "gx"),
        P("tracer", "gy", "gx"),
        P(None, "gy", "gx"),
        P("gy", "gx"),
        P("tracer"),
        P("gy", "gx"),
        P("gy", "gx"),
    )
    out_specs = (
        P("tracer", None, "gy", "gx"),
        P(None, "tracer", "gy", "gx"),
        P("tracer", "gy", "gx"),
    )
    body = functools.partial(per_device, mesh.shape["gx"], mesh.shape["gy"], mesh.shape["tracer"])
    return jax.shard_map(body, mesh=mesh, in_specs=in_specs, out_specs=out_specs, check_vma=False)
```

```python
import functools

import jax
import jax.numpy as jnp
from jax import lax
from jax.experimental import pallas as pl
from jax.experimental.pallas import tpu as pltpu
from jax.sharding import PartitionSpec as P

STEPS = 2
viscosity = 0.2
water_absorb = 0.04
plankton_absorb = 0.03
heat_share = 0.5
light_half = 0.3
nutrient_half = 0.5
SLOTS = 32
F32 = jnp.float32


def minmod(a, b):
    return jnp.maximum(jnp.minimum(a, b), jnp.minimum(jnp.maximum(a, b), 0.0))


def kernel(nx, ny, nt, NT, LV, LO, H, W,
           c_ref, flow_ref, temp_ref, kv_ref, sol_ref, eco_ref, ocean_ref, floor_ref, shift_ref,
           out_ref, outf_ref, outt_ref,
           cp1, cp2, xp1, xp2, xe1, xe2, xw1, xw2, hc, hs,
           flow_all, temp_all, flow_out, coef, part, arecv,
           fs, fr, hsend, hrecv, asend, arec_sem):
    gx, gy, t = lax.axis_index("gx"), lax.axis_index("gy"), lax.axis_index("tracer")
    WET, TF, UF, VF = 0, NT + 1, NT + 2, NT + 3
    G = H // SLOTS
    NCH = asend.shape[1]
    CH = H // NCH
    own = pl.multiple_of(t * (LO * H), 8)
    lane = lax.broadcasted_iota(jnp.int32, (LV, W), 1)
    level = lax.broadcasted_iota(jnp.int32, (LV, W), 0)
    lane_slot = lane // 4
    first, last = lane == 0, lane == W - 1
    half = (lane % 4) < 2
    sgn = jnp.where(half, 1.0, -1.0).astype(F32)

    has = (gy < ny - 1, gy > 0, gx < nx - 1, gx > 0)
    came = (gy > 0, gy < ny - 1, gx > 0, gx < nx - 1)
    peer = ({"gy": lax.rem(gy + 1, ny)}, {"gy": lax.rem(gy + ny - 1, ny)},
            {"gx": lax.rem(gx + 1, nx)}, {"gx": lax.rem(gx + nx - 1, nx)})
    barrier = pltpu.get_barrier_semaphore()
    for d in range(4):
        @pl.when(has[d])
        def _():
            pl.semaphore_signal(barrier, inc=1, device_id=peer[d], device_id_type=pl.DeviceIdType.MESH)
    for d in range(1, nt):
        pl.semaphore_signal(barrier, inc=1, device_id={"tracer": lax.rem(t + d, nt)},
                            device_id_type=pl.DeviceIdType.MESH)
    pl.semaphore_wait(barrier, sum(x.astype(jnp.int32) for x in has) + (nt - 1))

    def remote(src, dst, ss, rs, dev):
        return pltpu.make_async_remote_copy(src_ref=src, dst_ref=dst, send_sem=ss, recv_sem=rs,
                                            device_id=dev, device_id_type=pl.DeviceIdType.MESH)

    flows = [remote(flow_ref, flow_all.at[:, pl.ds(own, LO * H), :], fs.at[d], fr.at[d],
                    {"tracer": lax.rem(t + d, nt)}) for d in range(1, nt)]
    for cp in flows:
        cp.start()

    def exchange(step, grp, cp, xp, xe, xw, lo, n):
        f = pl.ds(lo, n)
        pairs = ((cp.at[f, pl.ds(H, 2)], cp.at[f, pl.ds(0, 2)]),
                 (cp.at[f, pl.ds(2, 2)], cp.at[f, pl.ds(H + 2, 2)]),
                 (xp.at[f], xw.at[f]), (xp.at[f], xe.at[f]))
        return [remote(s, r, hsend.at[step, grp, d], hrecv.at[step, grp, d], peer[d])
                for d, (s, r) in enumerate(pairs)]

    def start(copies, dirs):
        for d in dirs:
            @pl.when(has[d])
            def _():
                copies[d].start()

    def wait_recv(copies):
        for d in range(4):
            @pl.when(came[d])
            def _():
                copies[d].wait_recv()

    def wait_send(copies):
        for d in range(4):
            @pl.when(has[d])
            def _():
                copies[d].wait_send()

    def pack(cp, xp, lo, n):
        def body(f, _):
            for g in range(G):
                acc = jnp.zeros((LV, W), F32)
                for j in range(SLOTS):
                    row = cp[f, 2 + g * SLOTS + j]
                    acc = jnp.where(lane_slot == j, pltpu.roll(row, (4 * j + 2) % W, 1), acc)
                xp[f, g] = acc
            return 0
        lax.fori_loop(lo, lo + n, body, 0)

    def unpack(xp, xe, xw, lo, n):
        def body(f, _):
            for g in range(G):
                o, e, w = xp[f, g], xe[f, g], xw[f, g]
                near = jnp.where(half, pltpu.roll(e, W - 1, 1), pltpu.roll(w, 1, 1))
                far = jnp.where(half, pltpu.roll(e, W - 2, 1), pltpu.roll(w, 2, 1))
                hc[f, g] = near
                hs[f, g] = sgn * minmod(far - near, near - o)
            return 0
        lax.fori_loop(lo, lo + n, body, 0)

    def clear_edges(cp, xe, xw):
        NF = NT + 4
        zrow = jnp.zeros((NF, 2, LV, W), F32)
        zx = jnp.zeros((NF, G, LV, W), F32)
        @pl.when(gy == 0)
        def _():
            cp[:, 0:2] = zrow
        @pl.when(gy == ny - 1)
        def _():
            cp[:, H + 2:H + 4] = zrow
        @pl.when(gx == nx - 1)
        def _():
            xe[...] = zx
        @pl.when(gx == 0)
        def _():
            xw[...] = zx

    def each_row(lo, hi, n, fn):
        def body(i, _):
            for r in range(n):
                fn(i * n + r, 0)
            return 0
        lax.fori_loop(lo // n, hi // n, body, 0)

    def rows(ref, y):
        return ref[pl.ds(y, LV, stride=H), :]

    temp_all[...] = jnp.zeros((LV * H, W), F32)
    temp_all[pl.ds(own, LO * H), :] = temp_ref[...]
    flow_all[:, pl.ds(own, LO * H), :] = flow_ref[...]
    clear_edges(cp1, xe1, xw1)
    clear_edges(cp2, xe2, xw2)

    def load(y, _):
        depth = ocean_ref[pl.ds(y, 1), :] * floor_ref[pl.ds(y, 1), :]
        cp1[WET, y + 2] = jnp.where(level < jnp.broadcast_to(depth, (LV, W)), 1.0, 0.0).astype(F32)
        for k in range(NT):
            cp1[1 + k, y + 2] = rows(c_ref.at[k], y)
        cp1[TF, y + 2] = rows(temp_all, y)
        return 0
    each_row(0, H, 2, load)

    a1 = exchange(0, 0, cp1, xp1, xe1, xw1, 0, NT + 2)
    b1 = exchange(0, 1, cp1, xp1, xe1, xw1, UF, 2)
    a2 = exchange(1, 0, cp2, xp2, xe2, xw2, 1, NT + 1)
    b2 = exchange(1, 1, cp2, xp2, xe2, xw2, UF, 2)
    start(a1, (0, 1))
    pack(cp1, xp1, 0, NT + 2)
    start(a1, (2, 3))

    for cp in flows:
        cp.wait_recv()

    def load_flow(y, _):
        cp1[UF, y + 2] = rows(flow_all.at[0], y)
        cp1[VF, y + 2] = rows(flow_all.at[1], y)
        return 0
    each_row(0, H, 8, load_flow)
    start(b1, (0, 1))
    pack(cp1, xp1, UF, 2)
    start(b1, (2, 3))
    wait_recv(a1)
    unpack(xp1, xe1, xw1, 0, NT + 2)
    wait_recv(b1)
    unpack(xp1, xe1, xw1, UF, 2)

    grid_rows = H * ny

    def halo(ref, f, y):
        return pltpu.roll(ref[f, y // SLOTS], W - 2 - 4 * lax.rem(y, SLOTS), 1)

    def sides(q, h):
        return (jnp.where(last, h, pltpu.roll(q, W - 1, 1)), jnp.where(first, h, pltpu.roll(q, 1, 1)))

    def currents(cp, store):
        def body(y, _):
            wet, wn, ws = cp1[WET, y + 2], cp1[WET, y + 3], cp1[WET, y + 1]
            u, un, us = cp[UF, y + 2], cp[UF, y + 3], cp[UF, y + 1]
            v, vn, vs = cp[VF, y + 2], cp[VF, y + 3], cp[VF, y + 1]
            we = coef[14, y]
            ww = coef[15, y]
            ue, uw = sides(u, halo(hc, UF, y))
            ve, vw = sides(v, halo(hc, VF, y))
            oe, on = wet * we, wet * wn
            cor = 0.1 + 0.1 * (gy * H + y).astype(F32) / grid_rows
            lap_u = ue + uw + un + us - 4.0 * u
            lap_v = ve + vw + vn + vs - 4.0 * v
            store(y, oe * (u + cor * v + viscosity * lap_u), on * (v - cor * u + viscosity * lap_v))
            U, V = oe * u, on * v
            Uw, Vs = wet * ww * uw, wet * ws * vs
            pe, me, pw, mw = jnp.maximum(U, 0.0), jnp.minimum(U, 0.0), jnp.maximum(Uw, 0.0), jnp.minimum(Uw, 0.0)
            pn, mn, ps, ms = jnp.maximum(V, 0.0), jnp.minimum(V, 0.0), jnp.maximum(Vs, 0.0), jnp.minimum(Vs, 0.0)
            coef[0, y] = wet * (1.0 - pe + mw - pn + ms)
            coef[1, y] = -(wet * me)
            coef[2, y] = wet * pw
            coef[3, y] = -0.5 * wet * (pe * (1.0 - U) + mw * (1.0 + Uw))
            coef[4, y] = 0.5 * wet * me * (1.0 + U)
            coef[5, y] = 0.5 * wet * pw * (1.0 - Uw)
            coef[6, y] = -(wet * mn)
            coef[7, y] = wet * ps
            coef[8, y] = -0.5 * wet * (pn * (1.0 - V) + ms * (1.0 + Vs))
            coef[9, y] = 0.5 * wet * mn * (1.0 + V)
            coef[10, y] = 0.5 * wet * ps * (1.0 - Vs)
            return 0
        each_row(0, H, 4, body)

    def masks(y, _):
        wet = cp1[WET, y + 2]
        we, ww = sides(wet, halo(hc, WET, y))
        coef[14, y] = we
        coef[15, y] = ww
        below = jnp.where(level < LV - 1, pltpu.roll(wet, LV - 1, 0), 0.0)
        kv = rows(kv_ref, y) * wet * below
        up = pltpu.roll(kv, 1, 0)
        coef[11, y] = 1.0 - kv - up
        coef[12, y] = kv
        coef[13, y] = up
        return 0
    each_row(0, H, 8, masks)

    cells = (SLOTS, LV, W)
    flat = (SLOTS * LV, W)
    own_slot = lax.broadcasted_iota(jnp.int32, cells, 0) == lax.broadcasted_iota(jnp.int32, cells, 2) // 4

    def spread(edge):
        return jnp.where(own_slot, jnp.broadcast_to(edge[None], cells), 0.0).reshape(flat)

    def moved(x):
        return jnp.dot(x, shift_ref[...], preferred_element_type=F32)

    def advect(cp, dst, f, g, total):
        base = g * SLOTS
        c = cp[f, pl.ds(base + 2, SLOTS)].reshape(flat)
        x = jnp.concatenate([c, spread(hc[f, g])], 1)
        high = x.astype(jnp.bfloat16)
        low = (x - high.astype(F32)).astype(jnp.bfloat16)
        pair = moved(high) + moved(low)
        ce, cw = pair[:, :W], pair[:, W:]
        sx = minmod(ce - c, c - cw)
        spair = moved(jnp.concatenate([sx, spread(hs[f, g])], 1).astype(jnp.bfloat16))
        d = cp[f, pl.ds(base + 1, SLOTS + 3)] - cp[f, pl.ds(base, SLOTS + 3)]
        s = minmod(d[1:], d[:-1])
        for r in range(SLOTS):
            y, w = base + r, slice(r * LV, (r + 1) * LV)
            z = (coef[0, y] * c[w] + coef[1, y] * ce[w]) + (coef[2, y] * cw[w] + coef[3, y] * sx[w])
            z = z + (coef[4, y] * spair[w, :W] + coef[5, y] * spair[w, W:])
            z = z + (coef[6, y] * cp[f, y + 3] + coef[7, y] * cp[f, y + 1])
            adv = z + ((coef[8, y] * s[r + 1] + coef[9, y] * s[r + 2]) + coef[10, y] * s[r])
            m = coef[11, y] * adv + (coef[12, y] * pltpu.roll(adv, LV - 1, 0)
                                     + coef[13, y] * pltpu.roll(adv, 1, 0))
            dst[f, y + 2] = m
            if total is not None:
                part[total, y] = part[total, y] + m

    def tracers(cp, dst, step):
        sends = [[remote(part.at[step, pl.ds(q * CH, CH)], arecv.at[step, d - 1, pl.ds(q * CH, CH)],
                         asend.at[step, q, d], arec_sem.at[step, q, d],
                         {"tracer": lax.rem(t + d, nt)}) for d in range(1, nt)] for q in range(NCH)]
        part[step] = jnp.zeros((H, LV, W), F32)

        def plankton(i, _):
            advect(cp, dst, 2 + 3 * (i // G), lax.rem(i, G), step)
            return 0

        def others(i, _):
            q = i // G
            advect(cp, dst, 1 + 3 * (q // 2) + 2 * lax.rem(q, 2), lax.rem(i, G), None)
            return 0
        lax.fori_loop(0, NT // 3 * G, plankton, 0)
        for q in range(NCH):
            for cp_ in sends[q]:
                cp_.start()
        lax.fori_loop(0, NT // 3 * 2 * G, others, 0)
        return sends

    def ecology(cp, mix, step, sends, put, put_temp):
        rate = [eco_ref[k] for k in range(NT)]

        def body(y, _):
            total = part[step, y]
            for d in range(nt - 1):
                total = total + arecv[step, d, y]
            a = water_absorb + plankton_absorb * total
            acc = a
            for sh in (1, 2, 4):
                if sh < LV:
                    acc = acc + jnp.where(level >= sh, pltpu.roll(acc, sh, 0), 0.0)
            tau = acc - a
            sol = jnp.broadcast_to(sol_ref[pl.ds(y, 1), :], (LV, W))
            light = sol * jnp.exp(-tau - 0.5 * a)
            heat = heat_share * sol * (jnp.exp(-tau) - jnp.exp(-tau - a))
            lim = light / (light + light_half)
            wet = cp1[WET, y + 2]
            for k in range(0, NT, 3):
                n, p, dt = mix[1 + k, y + 2], mix[2 + k, y + 2], mix[3 + k, y + 2]
                uptake = (rate[k] * lim) * p * n / (jnp.abs(n) + nutrient_half)
                dead, back = rate[k + 1] * p, rate[k + 2] * dt
                put(k, y, wet * (n - uptake + back))
                put(k + 1, y, wet * (p + uptake - dead))
                put(k + 2, y, wet * (dt + dead - back))
            tm = cp[TF, y + 2]
            te, tw = sides(tm, halo(hc, TF, y))
            put_temp(y, coef[0, y] * tm + coef[1, y] * te + coef[2, y] * tw
                     + coef[6, y] * cp[TF, y + 3] + coef[7, y] * cp[TF, y + 1] + wet * heat)
            return 0
        for q in range(NCH):
            for cp_ in sends[q]:
                cp_.wait_recv()
            each_row(q * CH, (q + 1) * CH, 4, body)
        for q in range(NCH):
            for cp_ in sends[q]:
                cp_.wait_send()

    def store_next(y, u, v):
        cp2[UF, y + 2] = u
        cp2[VF, y + 2] = v
    currents(cp1, store_next)
    start(b2, (0, 1))
    pack(cp2, xp2, UF, 2)
    start(b2, (2, 3))
    sends = tracers(cp1, cp2, 0)

    def put_next(k, y, value):
        cp2[1 + k, y + 2] = value

    def put_temp_next(y, value):
        cp2[TF, y + 2] = value
    ecology(cp1, cp2, 0, sends, put_next, put_temp_next)
    start(a2, (0, 1))
    pack(cp2, xp2, 1, NT + 1)
    start(a2, (2, 3))

    wait_recv(b2)
    unpack(xp2, xe2, xw2, UF, 2)

    def store_last(y, u, v):
        flow_out[0, pl.ds(y, LV, stride=H), :] = u
        flow_out[1, pl.ds(y, LV, stride=H), :] = v
    currents(cp2, store_last)
    outf_ref[...] = flow_out[:, pl.ds(own, LO * H), :]
    wait_send(a1)
    wait_send(b1)
    for cp in flows:
        cp.wait_send()
    wait_recv(a2)
    unpack(xp2, xe2, xw2, 1, NT + 1)
    sends = tracers(cp2, cp1, 1)

    def put_last(k, y, value):
        out_ref[k, pl.ds(y, LV, stride=H), :] = value

    def put_temp_last(y, value):
        temp_all[pl.ds(y, LV, stride=H), :] = value
    ecology(cp2, cp1, 1, sends, put_last, put_temp_last)
    outt_ref[...] = temp_all[pl.ds(own, LO * H), :]
    wait_send(a2)
    wait_send(b2)


def shift_matrix(W):
    k, n = lax.broadcasted_iota(jnp.int32, (2 * W, 2 * W), 0), lax.broadcasted_iota(jnp.int32, (2 * W, 2 * W), 1)
    inside, edge = k < W, (k >= W)
    east = jnp.where(n < W - 1, inside & (k == n + 1), (n == W - 1) & edge & (k % 4 == 1))
    west = jnp.where(n > W, inside & (k == n - W - 1), (n == W) & edge & (k % 4 == 2))
    return jnp.where(n < W, east, west).astype(jnp.bfloat16)


def per_device(nx, ny, nt, c, flow, temp, kv, sol, eco, ocean, floor):
    NT, LV, H, W = c.shape
    LO = temp.shape[0]
    NF, G = NT + 4, H // SLOTS
    assert H % SLOTS == 0 and W == 4 * SLOTS
    NCH = 4
    vm = pltpu.VMEM
    dma = pltpu.SemaphoreType.DMA
    field = vm((NF, H + 4, LV, W), F32)
    edge = vm((NF, G, LV, W), F32)
    whole = pl.BlockSpec(memory_space=pltpu.VMEM)
    out, outf, outt = pl.pallas_call(
        functools.partial(kernel, nx, ny, nt, NT, LV, LO, H, W),
        out_shape=(jax.ShapeDtypeStruct((NT, LV * H, W), F32),
                   jax.ShapeDtypeStruct((2, LO * H, W), F32),
                   jax.ShapeDtypeStruct((LO * H, W), F32)),
        in_specs=[whole] * 5 + [pl.BlockSpec(memory_space=pltpu.SMEM)] + [whole] * 3,
        out_specs=(whole,) * 3,
        scratch_shapes=[field, field, edge, edge, edge, edge, edge, edge, edge, edge,
                        vm((2, LV * H, W), F32), vm((LV * H, W), F32), vm((2, LV * H, W), F32),
                        vm((16, H, LV, W), F32),
                        vm((STEPS, H, LV, W), F32), vm((STEPS, max(nt - 1, 1), H, LV, W), F32),
                        dma((nt,)), dma((nt,)), dma((STEPS, 2, 4)), dma((STEPS, 2, 4)),
                        dma((STEPS, NCH, nt)), dma((STEPS, NCH, nt))],
        compiler_params=pltpu.CompilerParams(collective_id=0, has_side_effects=True,
                                             vmem_limit_bytes=60 * 1024 * 1024),
        name="ocean",
    )(c.reshape(NT, LV * H, W), flow.reshape(2, LO * H, W), temp.reshape(LO * H, W),
      kv.reshape(LV * H, W), sol, eco, ocean, floor, shift_matrix(W))
    return out.reshape(c.shape), outf.reshape(flow.shape), outt.reshape(temp.shape)


def solution(mesh):
    in_specs = (
        P("tracer", None, "gy", "gx"),
        P(None, "tracer", "gy", "gx"),
        P("tracer", "gy", "gx"),
        P(None, "gy", "gx"),
        P("gy", "gx"),
        P("tracer"),
        P("gy", "gx"),
        P("gy", "gx"),
    )
    out_specs = (
        P("tracer", None, "gy", "gx"),
        P(None, "tracer", "gy", "gx"),
        P("tracer", "gy", "gx"),
    )
    body = functools.partial(per_device, mesh.shape["gx"], mesh.shape["gy"], mesh.shape["tracer"])
    return jax.shard_map(body, mesh=mesh, in_specs=in_specs, out_specs=out_specs, check_vma=False)
```

```python
import functools

import jax
import jax.numpy as jnp
from jax import lax
from jax.experimental import pallas as pl
from jax.experimental.pallas import tpu as pltpu
from jax.sharding import PartitionSpec as P

STEPS = 2
viscosity = 0.2
water_absorb = 0.04
plankton_absorb = 0.03
heat_share = 0.5
light_half = 0.3
nutrient_half = 0.5
SLOTS = 32
F32 = jnp.float32


def minmod(a, b):
    return jnp.maximum(jnp.minimum(a, b), jnp.minimum(jnp.maximum(a, b), 0.0))


def kernel(nx, ny, nt, NT, LV, LO, H, W,
           c_ref, flow_ref, temp_ref, kv_ref, sol_ref, eco_ref, ocean_ref, floor_ref, shift_ref, ends_ref,
           out_ref, outf_ref, outt_ref,
           cp1, cp2, xp1, xp2, xe1, xe2, xw1, xw2, hc, hs,
           flow_all, temp_all, flow_out, coef, part, arecv,
           fs, fr, hsend, hrecv, asend, arec_sem):
    gx, gy, t = lax.axis_index("gx"), lax.axis_index("gy"), lax.axis_index("tracer")
    WET, TF, UF, VF = 0, NT + 1, NT + 2, NT + 3
    G = H // SLOTS
    NCH = asend.shape[1]
    CH = H // NCH
    own = pl.multiple_of(t * (LO * H), 8)
    lane = lax.broadcasted_iota(jnp.int32, (LV, W), 1)
    level = lax.broadcasted_iota(jnp.int32, (LV, W), 0)
    lane_slot = lane // 4
    first, last = lane == 0, lane == W - 1
    half = (lane % 4) < 2
    sgn = jnp.where(half, 1.0, -1.0).astype(F32)

    has = (gy < ny - 1, gy > 0, gx < nx - 1, gx > 0)
    came = (gy > 0, gy < ny - 1, gx > 0, gx < nx - 1)
    peer = ({"gy": lax.rem(gy + 1, ny)}, {"gy": lax.rem(gy + ny - 1, ny)},
            {"gx": lax.rem(gx + 1, nx)}, {"gx": lax.rem(gx + nx - 1, nx)})
    barrier = pltpu.get_barrier_semaphore()
    for d in range(4):
        @pl.when(has[d])
        def _():
            pl.semaphore_signal(barrier, inc=1, device_id=peer[d], device_id_type=pl.DeviceIdType.MESH)
    for d in range(1, nt):
        pl.semaphore_signal(barrier, inc=1, device_id={"tracer": lax.rem(t + d, nt)},
                            device_id_type=pl.DeviceIdType.MESH)
    pl.semaphore_wait(barrier, sum(x.astype(jnp.int32) for x in has) + (nt - 1))

    def remote(src, dst, ss, rs, dev):
        return pltpu.make_async_remote_copy(src_ref=src, dst_ref=dst, send_sem=ss, recv_sem=rs,
                                            device_id=dev, device_id_type=pl.DeviceIdType.MESH)

    flows = [remote(flow_ref, flow_all.at[:, pl.ds(own, LO * H), :], fs.at[d], fr.at[d],
                    {"tracer": lax.rem(t + d, nt)}) for d in range(1, nt)]
    for cp in flows:
        cp.start()

    def exchange(step, grp, cp, xp, xe, xw, lo, n):
        f = pl.ds(lo, n)
        pairs = ((cp.at[f, pl.ds(H, 2)], cp.at[f, pl.ds(0, 2)]),
                 (cp.at[f, pl.ds(2, 2)], cp.at[f, pl.ds(H + 2, 2)]),
                 (xp.at[f], xw.at[f]), (xp.at[f], xe.at[f]))
        return [remote(s, r, hsend.at[step, grp, d], hrecv.at[step, grp, d], peer[d])
                for d, (s, r) in enumerate(pairs)]

    def start(copies, dirs):
        for d in dirs:
            @pl.when(has[d])
            def _():
                copies[d].start()

    def wait_recv(copies):
        for d in range(4):
            @pl.when(came[d])
            def _():
                copies[d].wait_recv()

    def wait_send(copies):
        for d in range(4):
            @pl.when(has[d])
            def _():
                copies[d].wait_send()

    def pack(cp, xp, lo, n):
        def body(f, _):
            for g in range(G):
                c = cp[f, pl.ds(2 + g * SLOTS, SLOTS)].reshape(SLOTS * LV, W)
                high = c.astype(jnp.bfloat16)
                low = (c - high.astype(F32)).astype(jnp.bfloat16)
                ends = jnp.dot(jnp.concatenate([high, low], 1), ends_ref[...], preferred_element_type=F32)
                acc = ends[:LV]
                for j in range(1, SLOTS):
                    acc = jnp.where(lane_slot == j, ends[j * LV:(j + 1) * LV], acc)
                xp[f, g] = acc
            return 0
        lax.fori_loop(lo, lo + n, body, 0)

    def unpack(xp, xe, xw, lo, n):
        def body(f, _):
            for g in range(G):
                o, e, w = xp[f, g], xe[f, g], xw[f, g]
                near = jnp.where(half, pltpu.roll(e, W - 1, 1), pltpu.roll(w, 1, 1))
                far = jnp.where(half, pltpu.roll(e, W - 2, 1), pltpu.roll(w, 2, 1))
                hc[f, g] = near
                hs[f, g] = sgn * minmod(far - near, near - o)
            return 0
        lax.fori_loop(lo, lo + n, body, 0)

    def clear_edges(cp, xe, xw):
        NF = NT + 4
        zrow = jnp.zeros((NF, 2, LV, W), F32)
        zx = jnp.zeros((NF, G, LV, W), F32)
        @pl.when(gy == 0)
        def _():
            cp[:, 0:2] = zrow
        @pl.when(gy == ny - 1)
        def _():
            cp[:, H + 2:H + 4] = zrow
        @pl.when(gx == nx - 1)
        def _():
            xe[...] = zx
        @pl.when(gx == 0)
        def _():
            xw[...] = zx

    def each_row(lo, hi, n, fn):
        def body(i, _):
            for r in range(n):
                fn(i * n + r, 0)
            return 0
        lax.fori_loop(lo // n, hi // n, body, 0)

    def rows(ref, y):
        return ref[pl.ds(y, LV, stride=H), :]

    temp_all[...] = jnp.zeros((LV * H, W), F32)
    temp_all[pl.ds(own, LO * H), :] = temp_ref[...]
    flow_all[:, pl.ds(own, LO * H), :] = flow_ref[...]
    clear_edges(cp1, xe1, xw1)
    clear_edges(cp2, xe2, xw2)

    def load(y, _):
        depth = ocean_ref[pl.ds(y, 1), :] * floor_ref[pl.ds(y, 1), :]
        cp1[WET, y + 2] = jnp.where(level < jnp.broadcast_to(depth, (LV, W)), 1.0, 0.0).astype(F32)
        for k in range(NT):
            cp1[1 + k, y + 2] = rows(c_ref.at[k], y)
        cp1[TF, y + 2] = rows(temp_all, y)
        return 0
    each_row(0, H, 2, load)

    a1 = exchange(0, 0, cp1, xp1, xe1, xw1, 0, NT + 2)
    b1 = exchange(0, 1, cp1, xp1, xe1, xw1, UF, 2)
    a2 = exchange(1, 0, cp2, xp2, xe2, xw2, 1, NT + 1)
    b2 = exchange(1, 1, cp2, xp2, xe2, xw2, UF, 2)
    start(a1, (0, 1))
    pack(cp1, xp1, 0, NT + 2)
    start(a1, (2, 3))

    for cp in flows:
        cp.wait_recv()

    def load_flow(y, _):
        cp1[UF, y + 2] = rows(flow_all.at[0], y)
        cp1[VF, y + 2] = rows(flow_all.at[1], y)
        return 0
    each_row(0, H, 8, load_flow)
    start(b1, (0, 1))
    pack(cp1, xp1, UF, 2)
    start(b1, (2, 3))
    wait_recv(a1)
    unpack(xp1, xe1, xw1, 0, NT + 2)
    wait_recv(b1)
    unpack(xp1, xe1, xw1, UF, 2)

    grid_rows = H * ny

    def halo(ref, f, y):
        return pltpu.roll(ref[f, y // SLOTS], W - 2 - 4 * lax.rem(y, SLOTS), 1)

    def sides(q, h):
        return (jnp.where(last, h, pltpu.roll(q, W - 1, 1)), jnp.where(first, h, pltpu.roll(q, 1, 1)))

    def currents(cp, store):
        def body(y, _):
            wet, wn, ws = cp1[WET, y + 2], cp1[WET, y + 3], cp1[WET, y + 1]
            u, un, us = cp[UF, y + 2], cp[UF, y + 3], cp[UF, y + 1]
            v, vn, vs = cp[VF, y + 2], cp[VF, y + 3], cp[VF, y + 1]
            we = coef[14, y]
            ww = coef[15, y]
            ue, uw = sides(u, halo(hc, UF, y))
            ve, vw = sides(v, halo(hc, VF, y))
            oe, on = wet * we, wet * wn
            cor = 0.1 + 0.1 * (gy * H + y).astype(F32) / grid_rows
            lap_u = ue + uw + un + us - 4.0 * u
            lap_v = ve + vw + vn + vs - 4.0 * v
            store(y, oe * (u + cor * v + viscosity * lap_u), on * (v - cor * u + viscosity * lap_v))
            U, V = oe * u, on * v
            Uw, Vs = wet * ww * uw, wet * ws * vs
            pe, me, pw, mw = jnp.maximum(U, 0.0), jnp.minimum(U, 0.0), jnp.maximum(Uw, 0.0), jnp.minimum(Uw, 0.0)
            pn, mn, ps, ms = jnp.maximum(V, 0.0), jnp.minimum(V, 0.0), jnp.maximum(Vs, 0.0), jnp.minimum(Vs, 0.0)
            coef[0, y] = wet * (1.0 - pe + mw - pn + ms)
            coef[1, y] = -(wet * me)
            coef[2, y] = wet * pw
            coef[3, y] = -0.5 * wet * (pe * (1.0 - U) + mw * (1.0 + Uw))
            coef[4, y] = 0.5 * wet * me * (1.0 + U)
            coef[5, y] = 0.5 * wet * pw * (1.0 - Uw)
            coef[6, y] = -(wet * mn)
            coef[7, y] = wet * ps
            coef[8, y] = -0.5 * wet * (pn * (1.0 - V) + ms * (1.0 + Vs))
            coef[9, y] = 0.5 * wet * mn * (1.0 + V)
            coef[10, y] = 0.5 * wet * ps * (1.0 - Vs)
            return 0
        each_row(0, H, 4, body)

    def masks(y, _):
        wet = cp1[WET, y + 2]
        we, ww = sides(wet, halo(hc, WET, y))
        coef[14, y] = we
        coef[15, y] = ww
        below = jnp.where(level < LV - 1, pltpu.roll(wet, LV - 1, 0), 0.0)
        kv = rows(kv_ref, y) * wet * below
        up = pltpu.roll(kv, 1, 0)
        coef[11, y] = 1.0 - kv - up
        coef[12, y] = kv
        coef[13, y] = up
        return 0
    each_row(0, H, 8, masks)

    cells = (SLOTS, LV, W)
    flat = (SLOTS * LV, W)
    own_slot = lax.broadcasted_iota(jnp.int32, cells, 0) == lax.broadcasted_iota(jnp.int32, cells, 2) // 4

    def spread(edge):
        return jnp.where(own_slot, jnp.broadcast_to(edge[None], cells), 0.0).reshape(flat)

    def moved(x):
        return jnp.dot(x, shift_ref[...], preferred_element_type=F32)

    def advect(cp, dst, f, g, total):
        base = g * SLOTS
        c = cp[f, pl.ds(base + 2, SLOTS)].reshape(flat)
        x = jnp.concatenate([c, spread(hc[f, g])], 1)
        high = x.astype(jnp.bfloat16)
        low = (x - high.astype(F32)).astype(jnp.bfloat16)
        pair = moved(high) + moved(low)
        ce, cw = pair[:, :W], pair[:, W:]
        sx = minmod(ce - c, c - cw)
        spair = moved(jnp.concatenate([sx, spread(hs[f, g])], 1).astype(jnp.bfloat16))
        d = cp[f, pl.ds(base + 1, SLOTS + 3)] - cp[f, pl.ds(base, SLOTS + 3)]
        s = minmod(d[1:], d[:-1])
        for r in range(SLOTS):
            y, w = base + r, slice(r * LV, (r + 1) * LV)
            z = (coef[0, y] * c[w] + coef[1, y] * ce[w]) + (coef[2, y] * cw[w] + coef[3, y] * sx[w])
            z = z + (coef[4, y] * spair[w, :W] + coef[5, y] * spair[w, W:])
            z = z + (coef[6, y] * cp[f, y + 3] + coef[7, y] * cp[f, y + 1])
            adv = z + ((coef[8, y] * s[r + 1] + coef[9, y] * s[r + 2]) + coef[10, y] * s[r])
            m = coef[11, y] * adv + (coef[12, y] * pltpu.roll(adv, LV - 1, 0)
                                     + coef[13, y] * pltpu.roll(adv, 1, 0))
            dst[f, y + 2] = m
            if total is not None:
                part[total, y] = part[total, y] + m

    def tracers(cp, dst, step):
        sends = [[remote(part.at[step, pl.ds(q * CH, CH)], arecv.at[step, d - 1, pl.ds(q * CH, CH)],
                         asend.at[step, q, d], arec_sem.at[step, q, d],
                         {"tracer": lax.rem(t + d, nt)}) for d in range(1, nt)] for q in range(NCH)]
        part[step] = jnp.zeros((H, LV, W), F32)

        def plankton(i, _):
            advect(cp, dst, 2 + 3 * (i // G), lax.rem(i, G), step)
            return 0

        def others(i, _):
            q = i // G
            advect(cp, dst, 1 + 3 * (q // 2) + 2 * lax.rem(q, 2), lax.rem(i, G), None)
            return 0
        lax.fori_loop(0, NT // 3 * G, plankton, 0)
        for q in range(NCH):
            for cp_ in sends[q]:
                cp_.start()
        lax.fori_loop(0, NT // 3 * 2 * G, others, 0)
        return sends

    def ecology(cp, mix, step, sends, put, put_temp):
        rate = [eco_ref[k] for k in range(NT)]

        def body(y, _):
            total = part[step, y]
            for d in range(nt - 1):
                total = total + arecv[step, d, y]
            a = water_absorb + plankton_absorb * total
            acc = a
            for sh in (1, 2, 4):
                if sh < LV:
                    acc = acc + jnp.where(level >= sh, pltpu.roll(acc, sh, 0), 0.0)
            tau = acc - a
            sol = jnp.broadcast_to(sol_ref[pl.ds(y, 1), :], (LV, W))
            light = sol * jnp.exp(-tau - 0.5 * a)
            heat = heat_share * sol * (jnp.exp(-tau) - jnp.exp(-tau - a))
            lim = light / (light + light_half)
            wet = cp1[WET, y + 2]
            for k in range(0, NT, 3):
                n, p, dt = mix[1 + k, y + 2], mix[2 + k, y + 2], mix[3 + k, y + 2]
                uptake = (rate[k] * lim) * p * n / (jnp.abs(n) + nutrient_half)
                dead, back = rate[k + 1] * p, rate[k + 2] * dt
                put(k, y, wet * (n - uptake + back))
                put(k + 1, y, wet * (p + uptake - dead))
                put(k + 2, y, wet * (dt + dead - back))
            tm = cp[TF, y + 2]
            te, tw = sides(tm, halo(hc, TF, y))
            put_temp(y, coef[0, y] * tm + coef[1, y] * te + coef[2, y] * tw
                     + coef[6, y] * cp[TF, y + 3] + coef[7, y] * cp[TF, y + 1] + wet * heat)
            return 0
        for q in range(NCH):
            for cp_ in sends[q]:
                cp_.wait_recv()
            each_row(q * CH, (q + 1) * CH, 4, body)
        for q in range(NCH):
            for cp_ in sends[q]:
                cp_.wait_send()

    def store_next(y, u, v):
        cp2[UF, y + 2] = u
        cp2[VF, y + 2] = v
    currents(cp1, store_next)
    start(b2, (0, 1))
    pack(cp2, xp2, UF, 2)
    start(b2, (2, 3))
    sends = tracers(cp1, cp2, 0)

    def put_next(k, y, value):
        cp2[1 + k, y + 2] = value

    def put_temp_next(y, value):
        cp2[TF, y + 2] = value
    ecology(cp1, cp2, 0, sends, put_next, put_temp_next)
    start(a2, (0, 1))
    pack(cp2, xp2, 1, NT + 1)
    start(a2, (2, 3))

    wait_recv(b2)
    unpack(xp2, xe2, xw2, UF, 2)

    def store_last(y, u, v):
        flow_out[0, pl.ds(y, LV, stride=H), :] = u
        flow_out[1, pl.ds(y, LV, stride=H), :] = v
    currents(cp2, store_last)
    outf_ref[...] = flow_out[:, pl.ds(own, LO * H), :]
    wait_send(a1)
    wait_send(b1)
    for cp in flows:
        cp.wait_send()
    wait_recv(a2)
    unpack(xp2, xe2, xw2, 1, NT + 1)
    sends = tracers(cp2, cp1, 1)

    def put_last(k, y, value):
        out_ref[k, pl.ds(y, LV, stride=H), :] = value

    def put_temp_last(y, value):
        temp_all[pl.ds(y, LV, stride=H), :] = value
    ecology(cp2, cp1, 1, sends, put_last, put_temp_last)
    outt_ref[...] = temp_all[pl.ds(own, LO * H), :]
    wait_send(a2)
    wait_send(b2)


def shift_matrix(W):
    k, n = lax.broadcasted_iota(jnp.int32, (2 * W, 2 * W), 0), lax.broadcasted_iota(jnp.int32, (2 * W, 2 * W), 1)
    inside, edge = k < W, (k >= W)
    east = jnp.where(n < W - 1, inside & (k == n + 1), (n == W - 1) & edge & (k % 4 == 1))
    west = jnp.where(n > W, inside & (k == n - W - 1), (n == W) & edge & (k % 4 == 2))
    return jnp.where(n < W, east, west).astype(jnp.bfloat16)


def ends_matrix(W):
    k, n = lax.broadcasted_iota(jnp.int32, (2 * W, W), 0), lax.broadcasted_iota(jnp.int32, (2 * W, W), 1)
    return (k % W == (n % 4 + W - 2) % W).astype(jnp.bfloat16)


def per_device(nx, ny, nt, c, flow, temp, kv, sol, eco, ocean, floor):
    NT, LV, H, W = c.shape
    LO = temp.shape[0]
    NF, G = NT + 4, H // SLOTS
    assert H % SLOTS == 0 and W == 4 * SLOTS
    NCH = 4
    vm = pltpu.VMEM
    dma = pltpu.SemaphoreType.DMA
    field = vm((NF, H + 4, LV, W), F32)
    edge = vm((NF, G, LV, W), F32)
    whole = pl.BlockSpec(memory_space=pltpu.VMEM)
    out, outf, outt = pl.pallas_call(
        functools.partial(kernel, nx, ny, nt, NT, LV, LO, H, W),
        out_shape=(jax.ShapeDtypeStruct((NT, LV * H, W), F32),
                   jax.ShapeDtypeStruct((2, LO * H, W), F32),
                   jax.ShapeDtypeStruct((LO * H, W), F32)),
        in_specs=[whole] * 5 + [pl.BlockSpec(memory_space=pltpu.SMEM)] + [whole] * 4,
        out_specs=(whole,) * 3,
        scratch_shapes=[field, field, edge, edge, edge, edge, edge, edge, edge, edge,
                        vm((2, LV * H, W), F32), vm((LV * H, W), F32), vm((2, LV * H, W), F32),
                        vm((16, H, LV, W), F32),
                        vm((STEPS, H, LV, W), F32), vm((STEPS, max(nt - 1, 1), H, LV, W), F32),
                        dma((nt,)), dma((nt,)), dma((STEPS, 2, 4)), dma((STEPS, 2, 4)),
                        dma((STEPS, NCH, nt)), dma((STEPS, NCH, nt))],
        compiler_params=pltpu.CompilerParams(collective_id=0, has_side_effects=True,
                                             vmem_limit_bytes=60 * 1024 * 1024),
        name="ocean",
    )(c.reshape(NT, LV * H, W), flow.reshape(2, LO * H, W), temp.reshape(LO * H, W),
      kv.reshape(LV * H, W), sol, eco, ocean, floor, shift_matrix(W), ends_matrix(W))
    return out.reshape(c.shape), outf.reshape(flow.shape), outt.reshape(temp.shape)


def solution(mesh):
    in_specs = (
        P("tracer", None, "gy", "gx"),
        P(None, "tracer", "gy", "gx"),
        P("tracer", "gy", "gx"),
        P(None, "gy", "gx"),
        P("gy", "gx"),
        P("tracer"),
        P("gy", "gx"),
        P("gy", "gx"),
    )
    out_specs = (
        P("tracer", None, "gy", "gx"),
        P(None, "tracer", "gy", "gx"),
        P("tracer", "gy", "gx"),
    )
    body = functools.partial(per_device, mesh.shape["gx"], mesh.shape["gy"], mesh.shape["tracer"])
    return jax.shard_map(body, mesh=mesh, in_specs=in_specs, out_specs=out_specs, check_vma=False)
```
